256 devices in a mesh: leaf: 4 (over x), front: 64 (over z, y, core).
Axes of the slice: x: 4, y: 4, z: 8, core: 2. Of those that a mesh axis runs over, the one named last changes fastest.
Arguments:
- front: float32 [16384, 16384], P('leaf', 'front'), as said below
- updates: float32 [8192, 128, 128], P(('leaf', 'front')), may hold values from -4 to 4
- target_owner: int32 [8192], P(('leaf', 'front')), may hold values from 0 to 63, as said below
- target_slot: int32 [8192], P(('leaf', 'front')), may hold values from 0 to 63
Outputs:
- factored: float32 [16384, 16384], P('leaf', 'front')
The draws below stay inside these ranges and needn't reach their ends.
Inputs may be any that keep to these rules, and one draw needn't show every extreme that they name: `target_owner`: among the 32 blocks of one device every owner index appears at most once; in every group of devices sharing an index of leaf, some owner index is named by every device of the group. The front is symmetric.
All inputs are finite; a program needn't handle non-finite values.
Results may differ from the reference program's by a relative error of at most 0.00015.
Values sent between devices are 32-bit elements; how exact they have to be, the bound alone decides.
A program may use at most 128 MiB of HBM per device.

```python
import jax
import jax.numpy as jnp
from jax import lax

W = 256
TILE = 128
SENDS = 32
M = 16384
BAND = 4096
TILES = 64
N_LEAF = 4
N_FRONT = 64


def draw_front(key, part):
    gram_key = jax.random.fold_in(key, 21)
    noise_key = jax.random.fold_in(key, 22)
    factor = jax.random.randint(gram_key, (M, W), -2, 3).astype(jnp.float32)
    spread = 2.0
    noise = jnp.clip(jax.random.normal(noise_key, (M, M), jnp.float32), -4.0, 4.0) * 0.3
    gram = jnp.dot(factor, factor.T, precision=lax.Precision.HIGHEST)
    balanced = 0.5 * (noise + noise.T)
    rows = jnp.arange(M, dtype=jnp.int32)
    shift = jnp.where(rows[:, None] == rows[None, :], jnp.float32(80.0), jnp.float32(0.0))
    return gram * jnp.float32(200.0 / (spread * W)) + balanced + shift


def draw_target_owner(key, part):
    senders = N_LEAF * N_FRONT
    common = jax.random.randint(jax.random.fold_in(key, 11), (N_LEAF,), 0, N_FRONT)

    def offsets(sub):
        picked = jax.random.permutation(sub, N_FRONT - 1)[:SENDS - 1].astype(jnp.int32) + 1
        return jnp.concatenate([jnp.zeros((1,), jnp.int32), picked])
    keys = jax.random.split(jax.random.fold_in(key, 12), senders)
    table = jax.vmap(offsets)(keys)
    base = jnp.repeat(common, N_FRONT)
    return ((base[:, None] + table) % N_FRONT).reshape(-1).astype(jnp.int32)


def place_ends(array, rng, low, high):
    longest = array.shape.index(max(array.shape))
    spots = []
    for shift in (0, 1):
        where = [jax.random.randint(jax.random.fold_in(rng, axis), (), 0, length) for axis, length in enumerate(array.shape)]
        where[longest] = (where[longest] + shift) % array.shape[longest]
        spots.append(tuple(where))
    return array.at[spots[0]].set(low).at[spots[1]].set(high)


def shard_levels(stream_key, dims, cuts, least, high):
    def one(position, parts):
        draws = jax.random.uniform(jax.random.fold_in(jax.random.fold_in(stream_key, 6), position), (parts,), jnp.float32, least / len(cuts), high / len(cuts))
        return jnp.repeat(jnp.exp(draws), dims[position] // parts).reshape((-1,) + (1,) * (len(dims) - position - 1))

    factor_of = one(*cuts[0])
    for cut in cuts[1:]:
        factor_of = factor_of * one(*cut)
    return factor_of


def centred(stream_key, dims, width, limit, cuts=(), kind=jnp.bfloat16):
    values = width * jax.random.normal(stream_key, dims, jnp.float32)
    if cuts:
        values = values * shard_levels(stream_key, dims, cuts, -0.22, 0.18)
    return jnp.clip(values, -limit, limit).astype(kind)


def setup_inputs(seed: int = 0) -> dict:
    arg_keys = jax.random.split(jax.random.key(seed), 5)
    return {
        "front": draw_front(jax.random.fold_in(arg_keys[4], 71), 0),
        "updates": centred(arg_keys[1], (N_LEAF * N_FRONT * SENDS, TILE, TILE), 0.5, 4.0, ((0, 256),), jnp.float32),
        "target_owner": draw_target_owner(jax.random.fold_in(arg_keys[4], 71), 0),
        "target_slot": place_ends(jax.random.randint(arg_keys[3], (N_LEAF * N_FRONT * SENDS,), 0, TILES), jax.random.fold_in(arg_keys[3], 1), 0, TILES - 1).astype(jnp.int32),
    }


def panel_step(matrix, start):
    diag = matrix[start:start + W, start:start + W]
    chol = jnp.linalg.cholesky(diag)
    eye = jnp.eye(W, dtype=jnp.float32)
    inverse = lax.linalg.triangular_solve(chol, eye, left_side=True, lower=True)
    panel = matrix[:, start:start + W]
    prod = jnp.dot(panel, inverse.T, precision=lax.Precision.HIGHEST)
    row_ids = jnp.arange(M, dtype=jnp.int32)
    lower = jnp.where(row_ids[:, None] >= start, prod, panel)
    trail = lower[start + W:]
    block = matrix[start + W:, start + W:] - jnp.dot(trail, trail.T, precision=lax.Precision.HIGHEST)
    matrix = matrix.at[start + W:, start + W:].set(block)
    return matrix.at[:, start:start + W].set(lower)

def reference(front, updates, target_owner, target_slot):
    row_tiles = BAND // TILE
    col_tiles = W // TILE
    total = N_LEAF * N_FRONT * SENDS
    group = jnp.arange(total, dtype=jnp.int32) // (N_FRONT * SENDS)
    grow = group * row_tiles + target_slot // col_tiles
    gcol = target_owner * col_tiles + target_slot % col_tiles
    grid = front.reshape(M // TILE, TILE, M // TILE, TILE)
    grid = grid.at[grow, :, gcol, :].add(updates)
    matrix = grid.reshape(M, M)
    matrix = panel_step(matrix, 0)
    matrix = panel_step(matrix, W)
    return matrix
```

```python
import functools
import jax
import jax.numpy as jnp
from jax import lax
from jax.experimental import pallas as pl
from jax.experimental.pallas import tpu as pltpu
from jax.sharding import PartitionSpec as P

HI = lax.Precision.HIGHEST
def sort_kernel(owner_ref, slot_ref, updates_ref, top_ref, big_ref, small_ref, turned_ref, place_ref, sem):
    sends = updates_ref.shape[0]
    peers = big_ref.shape[0]
    tile = 128

    def send(j, carry):
        pltpu.make_async_copy(updates_ref.at[j], big_ref.at[owner_ref[j]], sem).start()
        return carry

    lax.fori_loop(0, sends, send, 0)

    def clear(d, carry):
        place_ref[d] = -1
        return carry

    lax.fori_loop(0, peers, clear, 0)

    def mark(j, carry):
        place_ref[owner_ref[j]] = j
        return carry

    lax.fori_loop(0, sends, mark, 0)

    def label(d):
        j = place_ref[d]
        return jnp.where(j >= 0, slot_ref[jnp.maximum(j, 0)], -1).astype(jnp.float32)

    row = lax.broadcasted_iota(jnp.int32, (8, tile), 0)
    for o in range(2):
        j = place_ref[o]
        block = jnp.where(j >= 0, updates_ref[jnp.maximum(j, 0)], 0.0)
        near = label(o)
        for a in range(16):
            for h in range(2):
                d = 4 * a + 2 * o + h
                small_ref[d, 0:8, :] = block[8 * a : 8 * a + 8, :]
                small_ref[d, 8:16, :] = jnp.where(row == 0, near, label(d))
    turned_ref[...] = top_ref[...].T
    pltpu.make_async_copy(updates_ref, big_ref.at[pl.ds(0, sends)], sem).wait()


def sort_blocks(owner, slot, updates, front, peers):
    f32 = jnp.float32
    width = front.shape[1]
    sends, tile = updates.shape[:2]
    smem = pl.BlockSpec(memory_space=pltpu.SMEM)
    vm = pl.BlockSpec(memory_space=pltpu.VMEM)
    return pl.pallas_call(
        sort_kernel,
        grid=(1,),
        out_shape=(
            jax.ShapeDtypeStruct((peers, tile, tile), f32),
            jax.ShapeDtypeStruct((peers, 16, tile), f32),
            jax.ShapeDtypeStruct((width, 2 * width), f32),
        ),
        in_specs=[smem, smem, pl.BlockSpec((sends, tile, tile), lambda i: (0, 0, 0)), pl.BlockSpec((2 * width, width), lambda i: (0, 0))],
        out_specs=(
            pl.BlockSpec(memory_space=pl.ANY),
            pl.BlockSpec((peers, 16, tile), lambda i: (0, 0, 0)),
            pl.BlockSpec((width, 2 * width), lambda i: (0, 0)),
        ),
        scratch_shapes=[pltpu.SMEM((peers,), jnp.int32), pltpu.SemaphoreType.DMA],
        name="sort_blocks",
    )(owner, slot, updates, front)


def split(x):
    high = x.astype(jnp.bfloat16)
    return high, (x - high.astype(jnp.float32)).astype(jnp.bfloat16)


def product(a, b):
    ah, al = split(a)
    bh, bl = b
    f32 = jnp.float32
    return (
        jnp.dot(ah, bh, preferred_element_type=f32)
        + jnp.dot(ah, bl, preferred_element_type=f32)
        + jnp.dot(al, bh, preferred_element_type=f32)
    )


def finish_kernel(where_ref, label_ref, front_ref, panel_ref, arrived_ref, high_ref, low_ref, out_ref, total_ref):
    step = pl.program_id(0)
    tile = 128

    @pl.when(step == 0)
    def _():
        total_ref[...] = jnp.zeros_like(total_ref)

        def add(j, carry):
            slot = label_ref[j]

            @pl.when(slot >= 0)
            def _():
                total_ref[slot] += arrived_ref[j]

            return carry

        lax.fori_loop(0, arrived_ref.shape[0], add, 0)

    column, band = where_ref[0], where_ref[1]
    kind = jnp.where(band == 0, jnp.minimum(step, 2), 2)
    minus = product(panel_ref[...], (high_ref[kind], low_ref[kind]))
    keep = jnp.logical_or(column >= 2, jnp.logical_and(column == 1, kind == 0))
    for h in range(2):
        for k in range(2):
            rows = slice(h * tile, h * tile + tile)
            cols = slice(k * tile, k * tile + tile)
            base = front_ref[rows, cols] + total_ref[step * 4 + h * 2 + k]
            out_ref[rows, cols] = jnp.where(keep, base, 0.0) - minus[rows, cols]


def finish(where, labels, front, panel, arrived, high, low):
    nrows, width = front.shape
    peers, tile = arrived.shape[:2]
    smem = pl.BlockSpec(memory_space=pltpu.SMEM)
    one = pl.Buffered(buffer_count=1)
    return pl.pallas_call(
        finish_kernel,
        grid=(nrows // 256,),
        out_shape=jax.ShapeDtypeStruct((nrows, width), jnp.float32),
        in_specs=[
            smem,
            smem,
            pl.BlockSpec((256, width), lambda i: (i, 0)),
            pl.BlockSpec((256, 2 * width), lambda i: (i, 0)),
            pl.BlockSpec(arrived.shape, lambda i: (0, 0, 0), pipeline_mode=one),
            pl.BlockSpec(high.shape, lambda i: (0, 0, 0), pipeline_mode=one),
            pl.BlockSpec(low.shape, lambda i: (0, 0, 0), pipeline_mode=one),
        ],
        out_specs=pl.BlockSpec((256, width), lambda i: (i, 0)),
        scratch_shapes=[pltpu.VMEM((64, tile, tile), jnp.float32)],
        name="finish",
    )(where, labels, front, panel, arrived, high, low)


NZ, NY, NC = 8, 4, 2


def panel_kernel(leafs, small_ref, turned_ref, panel_ref, diag_ref, mine_ref, got_ref, old_ref, part_ref, sems):
    peers = got_ref.shape[0]
    tile = 128
    x = lax.axis_index("leaf")
    f = lax.axis_index("front")
    z, y, c = f // (NY * NC), (f // NC) % NY, f % NC
    a, q = f // 4, f % 4
    half = y // 2

    def lanes(index):
        return pl.ds(pl.multiple_of(index * tile, tile), tile)

    def device(z2, y2, c2):
        return (z2 * NY + y2) * NC + c2

    def remote(src, dst, stage, target):
        pltpu.make_async_remote_copy(
            src_ref=src, dst_ref=dst, send_sem=sems.at[0, stage], recv_sem=sems.at[1, stage],
            device_id=target, device_id_type=pl.DeviceIdType.MESH,
        ).start()

    def local(src, dst, stage):
        pltpu.make_async_copy(src, dst, sems.at[1, stage]).start()

    def wait(ref, which, stage):
        pltpu.make_async_copy(ref, ref, sems.at[which, stage]).wait()

    local(small_ref.at[f], got_ref.at[f], 0)

    def send_slices(k, carry):
        d = lax.rem(f + k, peers)
        remote(small_ref.at[d], got_ref.at[f], 0, (x, d))
        return carry

    lax.fori_loop(1, peers, send_slices, 0)

    band, place = f // 16, f % 16

    @pl.when(x == 0)
    def _():
        def send_old(k, carry):
            i = lax.rem(f + k, peers)
            src = turned_ref.at[:, i // 4, :, lanes(i % 4)]
            dst = old_ref.at[pl.ds(2 * place, 2)]
            self_ = jnp.logical_and(band == 0, i == f)

            @pl.when(self_)
            def _():
                local(src, dst, 1)

            @pl.when(jnp.logical_not(self_))
            def _():
                remote(src, dst, 1, (band, i))

            return carry

        lax.fori_loop(0, peers, send_old, 0)

    wait(got_ref, 1, 0)
    wait(old_ref, 1, 1)

    slot = got_ref[:, 8, :]
    want = (2 * lax.broadcasted_iota(jnp.int32, (peers, tile), 1) + q % 2).astype(jnp.float32)
    pick = jnp.where(slot == want, 1.0, 0.0)
    for r in range(8):
        add = lax.dot_general(pick, got_ref[:, r, :], (((0,), (0,)), ((), ())), precision=HI, preferred_element_type=jnp.float32)
        part_ref[:, r, :] = old_ref[:, r, :] + add[0:32]

    panel_mine = panel_ref.at[:, z, half, :, lanes(q)]
    diag_mine = diag_ref.at[:, z, half, :, lanes(q)]
    local(part_ref, panel_mine, 2)

    @pl.when(x == 0)
    def _():
        local(part_ref.at[0:4], diag_mine, 3)

        def send_x(k, carry):
            remote(part_ref.at[0:4], diag_mine, 3, (k, f))
            return carry

        lax.fori_loop(1, leafs, send_x, 0)

    wait(diag_mine, 1, 3)
    wait(panel_mine, 1, 2)

    def along_z(ref, stage):
        def go(k, carry):
            view = ref.at[:, z, half, :, lanes(q)]
            remote(view, view, stage, (x, device(lax.rem(z + k, NZ), y, c)))
            return carry

        lax.fori_loop(1, NZ, go, 0)

    def along_y(ref, stage):
        def go(k, carry):
            view = ref.at[:, :, half, :, lanes(q)]
            remote(view, view, stage, (x, device(z, lax.rem(y + k, NY), c)))
            return carry

        lax.fori_loop(1, NY, go, 0)

    def across(ref, stage):
        for h in range(2):
            view = ref.at[:, :, :, :, lanes(2 * h + c)]
            remote(view, view, stage, (x, device(z, y, 1 - c)))

    def views(ref, axis):
        if axis == 0:
            return ref.at[:, pl.ds(0, NZ - 1), half, :, lanes(q)]
        if axis == 1:
            return ref.at[:, :, 0, :, pl.ds(0, (NY - 1) * tile)]
        return ref.at[:, :, :, :, pl.ds(0, 2 * tile)]

    along_z(diag_ref, 4)
    along_z(panel_ref, 5)
    wait(views(diag_ref, 0), 1, 4)
    along_y(diag_ref, 6)
    wait(views(diag_ref, 1), 1, 6)
    across(diag_ref, 8)
    wait(views(panel_ref, 0), 1, 5)
    along_y(panel_ref, 7)
    wait(views(diag_ref, 2), 1, 8)
    wait(views(panel_ref, 1), 1, 7)
    across(panel_ref, 9)
    wait(views(panel_ref, 2), 1, 9)

    rows = panel_ref.at[pl.ds(2 * place, 2)]

    @pl.when(x == band)
    def _():
        local(rows, mine_ref, 10)

        def send_rows(k, carry):
            remote(rows, mine_ref, 10, (lax.rem(x + k, leafs), f))
            return carry

        lax.fori_loop(1, leafs, send_rows, 0)

    wait(mine_ref, 1, 10)

    wait(small_ref.at[pl.ds(0, peers - 1)], 0, 0)

    @pl.when(x == 0)
    def _():
        @pl.when(band == 0)
        def _():
            wait(turned_ref.at[:, pl.ds(0, 15), :, :], 0, 1)
            wait(turned_ref.at[:, 0, :, pl.ds(0, 3 * tile)], 0, 1)

        @pl.when(band != 0)
        def _():
            wait(turned_ref, 0, 1)

        wait(part_ref.at[pl.ds(0, 4 * (leafs - 1))], 0, 3)

    wait(views(diag_ref, 0), 0, 4)
    wait(views(panel_ref, 0), 0, 5)
    wait(views(diag_ref, 1), 0, 6)
    wait(views(panel_ref, 1), 0, 7)
    wait(views(diag_ref, 2), 0, 8)
    wait(views(panel_ref, 2), 0, 9)

    @pl.when(x == band)
    def _():
        wait(panel_ref.at[pl.ds(0, 2 * (leafs - 1))], 0, 10)


def panels(mesh_shape, small, turned):
    f32 = jnp.float32
    leafs, peers = mesh_shape["leaf"], mesh_shape["front"]
    vm = pl.BlockSpec(memory_space=pltpu.VMEM)
    panel, diag, mine, got = pl.pallas_call(
        functools.partial(panel_kernel, leafs),
        out_shape=(
            jax.ShapeDtypeStruct((32, NZ, 2, 8, 512), f32),
            jax.ShapeDtypeStruct((4, NZ, 2, 8, 512), f32),
            jax.ShapeDtypeStruct((2, NZ, 2, 8, 512), f32),
            jax.ShapeDtypeStruct((peers, 16, 128), f32),
        ),
        in_specs=[vm, vm],
        out_specs=(vm, vm, vm, vm),
        scratch_shapes=[
            pltpu.VMEM((32, 8, 128), f32),
            pltpu.VMEM((32, 8, 128), f32),
            pltpu.SemaphoreType.DMA((2, 11)),
        ],
        compiler_params=pltpu.CompilerParams(has_side_effects=True),
        name="panels",
    )(small, turned.reshape(2, 16, 8, 512))
    return panel.reshape(4096, 512), diag.reshape(512, 512), mine.reshape(256, 512), got


def dot(a, b, ca=1, cb=0):
    return lax.dot_general(a, b, (((ca,), (cb,)), ((), ())), precision=HI, preferred_element_type=jnp.float32)


def factor_inverse(a, m_ref, out_ref):
    n = 128
    row = lax.broadcasted_iota(jnp.int32, (n, n), 0)
    col = lax.broadcasted_iota(jnp.int32, (n, n), 1)
    m_ref[:, 0:n] = a
    m_ref[:, n : 2 * n] = jnp.where(row == col, 1.0, 0.0)
    sub = lax.broadcasted_iota(jnp.int32, (8, n), 0)
    lane = lax.broadcasted_iota(jnp.int32, (8, n), 1)

    def group(g, carry):
        start = pl.multiple_of(g * 8, 8)
        left = m_ref[pl.ds(start, 8), 0:n]
        right = m_ref[pl.ds(start, 8), n : 2 * n]
        cols = [jnp.broadcast_to(left[:, k : k + 1], (8, n)) for k in range(8)]
        scale = jnp.ones((8, n), jnp.float32)
        for j in range(8):
            pivot = jnp.broadcast_to(cols[j][j : j + 1, :], (8, n))
            below = jnp.where(sub > j, cols[j], 0.0) / pivot
            scale = jnp.where(sub == j, pivot, scale)
            for k in range(j + 1, 8):
                cols[k] = cols[k] - below * jnp.broadcast_to(cols[k][j : j + 1, :], (8, n))
            left = left - below * jnp.broadcast_to(left[j : j + 1, :], (8, n))
            right = right - below * jnp.broadcast_to(right[j : j + 1, :], (8, n))
        scale = lax.rsqrt(scale)
        left = left * scale
        right = right * scale
        out_ref[pl.ds(start, 8), :] = right
        turned = pltpu.roll(left, start, axis=1)
        turned = jnp.where(lane >= start + 8, turned, 0.0)
        m_ref[:, 0:n] = pltpu.roll(m_ref[:, 0:n] - dot(turned, left, 0, 0), n - 8, axis=1)
        m_ref[:, n : 2 * n] = m_ref[:, n : 2 * n] - dot(turned, right, 0, 0)
        return carry

    lax.fori_loop(0, n // 8, group, 0)


def factor_inverse_256(a, m_ref, p_ref, q_ref, out_ref):
    n = 128
    factor_inverse(a[:n, :n], m_ref, p_ref)
    p = p_ref[...]
    low = dot(a[n:, :n], p, 1, 1)
    factor_inverse(a[n:, n:] - dot(low, low, 1, 1), m_ref, q_ref)
    q = q_ref[...]
    out_ref[:n, :n] = p
    out_ref[:n, n:] = jnp.zeros((n, n), jnp.float32)
    out_ref[n:, n:] = q
    out_ref[n:, :n] = -dot(q, dot(low, p))


def weights_kernel(where_ref, d_ref, xc_ref, high_ref, low_ref, m_ref, p_ref, q_ref, c1_ref, c2_ref):
    w = 256
    column = where_ref[0]
    d11 = d_ref[0:w, 0:w]
    factor_inverse_256(0.5 * (d11 + d11.T), m_ref, p_ref, q_ref, c1_ref)
    c1 = c1_ref[...]
    low = dot(d_ref[w:, 0:w], c1, 1, 1)
    d22 = d_ref[w:, w:] - dot(low, low, 1, 1)
    factor_inverse_256(0.5 * (d22 + d22.T), m_ref, p_ref, q_ref, c2_ref)
    c2 = c2_ref[...]
    b = dot(c1, low, 0, 1)
    lc1 = dot(xc_ref[:, 0:w], c1, 1, 1)
    lc2 = dot(xc_ref[:, w:] - dot(lc1, low, 1, 1), c2, 1, 1)
    w1 = dot(c1, lc1, 0, 1)
    w2 = dot(c2, lc2, 0, 1)
    row = lax.broadcasted_iota(jnp.int32, (w, w), 0)
    col = lax.broadcasted_iota(jnp.int32, (w, w), 1)
    eye = jnp.where(row == col, 1.0, 0.0)
    first = column == 0
    second = column == 1
    c1t = dot(c1, eye, 0, 0)
    c2t = dot(c2, eye, 0, 0)
    w1 = jnp.where(first, -c1t, w1)
    w2 = jnp.where(second, -c2t, w2)
    none = jnp.zeros((w, w), jnp.float32)

    def put(kind, rows, value):
        high_ref[kind, rows, :], low_ref[kind, rows, :] = split(value)

    w2 = jnp.where(first, none, w2)
    top = jnp.where(first, w1, jnp.where(second, -dot(b, w2), w1 - dot(b, w2)))
    put(0, slice(0, w), jnp.where(first, w1, none))
    put(0, slice(w, 2 * w), none)
    put(1, slice(0, w), jnp.where(second, top, w1))
    put(1, slice(w, 2 * w), jnp.where(second, w2, none))
    put(2, slice(0, w), top)
    put(2, slice(w, 2 * w), w2)


def weights(column, d, xc):
    w = 256
    f32 = jnp.float32
    vm = pl.BlockSpec(memory_space=pltpu.VMEM)
    return pl.pallas_call(
        weights_kernel,
        out_shape=(jax.ShapeDtypeStruct((3, 2 * w, w), jnp.bfloat16),) * 2,
        in_specs=[pl.BlockSpec(memory_space=pltpu.SMEM), vm, vm],
        out_specs=(vm, vm),
        scratch_shapes=[
            pltpu.VMEM((128, 256), f32),
            pltpu.VMEM((128, 128), f32),
            pltpu.VMEM((128, 128), f32),
            pltpu.VMEM((w, w), f32),
            pltpu.VMEM((w, w), f32),
        ],
        name="weights",
    )(column, d, xc)


def shards(mesh_shape, front, updates, target_owner, target_slot):
    peers = mesh_shape["front"]
    big, small, turned = sort_blocks(target_owner, target_slot, updates, front, peers)
    arrived = lax.all_to_all(big, "front", split_axis=0, concat_axis=0, tiled=True)
    panel, diag, mine, got = panels(mesh_shape, small, turned)
    column = lax.axis_index("front").astype(jnp.int32)
    band = lax.axis_index("leaf").astype(jnp.int32)
    where = jnp.stack([column, band])
    labels = got[:, 9, 0].astype(jnp.int32)
    high, low = weights(where, diag, mine)
    return finish(where, labels, front, panel, arrived, high, low)


def solution(mesh):
    return jax.shard_map(
        functools.partial(shards, dict(mesh.shape)),
        mesh=mesh,
        in_specs=(
            P("leaf", "front"),
            P(("leaf", "front"), None, None),
            P(("leaf", "front")),
            P(("leaf", "front")),
        ),
        out_specs=P("leaf", "front"),
        check_vma=False,
    )
```

```python
import functools
import jax
import jax.numpy as jnp
from jax import lax
from jax.experimental import pallas as pl
from jax.experimental.pallas import tpu as pltpu
from jax.sharding import PartitionSpec as P

HI = lax.Precision.HIGHEST
def sort_kernel(owner_ref, slot_ref, updates_ref, top_ref, big_ref, small_ref, turned_ref, place_ref, sem):
    sends = updates_ref.shape[0]
    peers = big_ref.shape[0]
    tile = 128

    def send(j, carry):
        pltpu.make_async_copy(updates_ref.at[j], big_ref.at[owner_ref[j]], sem).start()
        return carry

    lax.fori_loop(0, sends, send, 0)

    def clear(d, carry):
        place_ref[d] = -1
        return carry

    lax.fori_loop(0, peers, clear, 0)

    def mark(j, carry):
        place_ref[owner_ref[j]] = j
        return carry

    lax.fori_loop(0, sends, mark, 0)

    def label(d):
        j = place_ref[d]
        return jnp.where(j >= 0, slot_ref[jnp.maximum(j, 0)], -1).astype(jnp.float32)

    row = lax.broadcasted_iota(jnp.int32, (8, tile), 0)
    for o in range(2):
        j = place_ref[o]
        block = jnp.where(j >= 0, updates_ref[jnp.maximum(j, 0)], 0.0)
        near = label(o)
        for a in range(16):
            for h in range(2):
                d = 4 * a + 2 * o + h
                small_ref[d, 0:8, :] = block[8 * a : 8 * a + 8, :]
                small_ref[d, 8:16, :] = jnp.where(row == 0, near, label(d))
    turned_ref[...] = top_ref[...].T
    pltpu.make_async_copy(updates_ref, big_ref.at[pl.ds(0, sends)], sem).wait()


def sort_blocks(owner, slot, updates, front, peers):
    f32 = jnp.float32
    width = front.shape[1]
    sends, tile = updates.shape[:2]
    smem = pl.BlockSpec(memory_space=pltpu.SMEM)
    vm = pl.BlockSpec(memory_space=pltpu.VMEM)
    return pl.pallas_call(
        sort_kernel,
        grid=(1,),
        out_shape=(
            jax.ShapeDtypeStruct((peers, tile, tile), f32),
            jax.ShapeDtypeStruct((peers, 16, tile), f32),
            jax.ShapeDtypeStruct((width, 2 * width), f32),
        ),
        in_specs=[smem, smem, pl.BlockSpec((sends, tile, tile), lambda i: (0, 0, 0)), pl.BlockSpec((2 * width, width), lambda i: (0, 0))],
        out_specs=(
            pl.BlockSpec(memory_space=pl.ANY),
            pl.BlockSpec((peers, 16, tile), lambda i: (0, 0, 0)),
            pl.BlockSpec((width, 2 * width), lambda i: (0, 0)),
        ),
        scratch_shapes=[pltpu.SMEM((peers,), jnp.int32), pltpu.SemaphoreType.DMA],
        name="sort_blocks",
    )(owner, slot, updates, front)


def split(x):
    high = x.astype(jnp.bfloat16)
    return high, (x - high.astype(jnp.float32)).astype(jnp.bfloat16)


def product(a, b):
    ah, al = split(a)
    bh, bl = b
    f32 = jnp.float32
    return (
        jnp.dot(ah, bh, preferred_element_type=f32)
        + jnp.dot(ah, bl, preferred_element_type=f32)
        + jnp.dot(al, bh, preferred_element_type=f32)
    )


def finish_kernel(label_ref, rest_ref, arrived_ref, out_ref, total_ref):
    step = pl.program_id(0)
    tile = 128
    column = lax.axis_index("front")
    band = lax.axis_index("leaf")

    @pl.when(step == 0)
    def _():
        total_ref[...] = jnp.zeros_like(total_ref)

        def add(j, carry):
            slot = label_ref[j, 0]

            @pl.when(slot >= 0)
            def _():
                total_ref[slot] += arrived_ref[j]

            return carry

        lax.fori_loop(0, arrived_ref.shape[0], add, 0)

    top = jnp.logical_and(band == 0, step == 0)
    for h in range(4):
        for k in range(2):
            rows = slice(h * tile, h * tile + tile)
            cols = slice(k * tile, k * tile + tile)
            keep = jnp.logical_or(column >= 2, jnp.logical_and(column == 1, jnp.logical_and(top, h < 2)))
            out_ref[rows, cols] = rest_ref[rows, cols] + jnp.where(keep, total_ref[step * 8 + h * 2 + k], 0.0)


def finish(labels, rest, arrived):
    nrows, width = rest.shape
    peers, tile = arrived.shape[:2]
    return pl.pallas_call(
        finish_kernel,
        grid=(nrows // 512,),
        out_shape=jax.ShapeDtypeStruct((nrows, width), jnp.float32),
        in_specs=[
            pl.BlockSpec(memory_space=pltpu.SMEM),
            pl.BlockSpec((512, width), lambda i: (i, 0)),
            pl.BlockSpec(arrived.shape, lambda i: (0, 0, 0), pipeline_mode=pl.Buffered(buffer_count=1)),
        ],
        out_specs=pl.BlockSpec((512, width), lambda i: (i, 0)),
        scratch_shapes=[pltpu.VMEM((64, tile, tile), jnp.float32)],
        name="finish",
    )(labels, rest, arrived)


MESH = pl.DeviceIdType.MESH
NZ, NY, NC = 8, 4, 2


def panel_kernel(
    leafs, plan, big_ref, small_ref, turned_ref, front_ref, rest_ref, arrived_ref, label_ref,
    panel_ref, diag_ref, mine_ref, got_ref, old_ref, part_ref, high_ref, low_ref, m_ref, p_ref, q_ref, c1_ref, c2_ref, sems,
):
    peers = got_ref.shape[0]
    tile = 128
    x = lax.axis_index("leaf")
    f = lax.axis_index("front")
    z, y, c = f // (NY * NC), (f // NC) % NY, f % NC
    a, q = f // 4, f % 4
    half = y // 2

    def lanes(index):
        return pl.ds(pl.multiple_of(index * tile, tile), tile)

    def device(z2, y2, c2):
        return (z2 * NY + y2) * NC + c2

    def remote(src, dst, stage, target):
        pltpu.make_async_remote_copy(
            src_ref=src, dst_ref=dst, send_sem=sems.at[0, stage], recv_sem=sems.at[1, stage],
            device_id=target, device_id_type=MESH,
        ).start()

    def local(src, dst, stage):
        pltpu.make_async_copy(src, dst, sems.at[1, stage]).start()

    def wait(ref, which, stage):
        pltpu.make_async_copy(ref, ref, sems.at[which, stage]).wait()

    barrier = pltpu.get_barrier_semaphore()
    total = leafs * peers
    me = x * peers + f

    def greet(k, carry):
        d = lax.rem(me + k, total)
        pl.semaphore_signal(barrier, inc=1, device_id=(d // peers, d % peers), device_id_type=MESH)
        return carry

    lax.fori_loop(1, total, greet, 0)
    pl.semaphore_wait(barrier, total - 1)

    def send_blocks(point):
        first, last = plan.get(point, (0, 0))

        def go(k, carry):
            d = lax.rem(f + k, peers)
            remote(big_ref.at[d], arrived_ref.at[f], 11, (x, d))
            return carry

        if last > first:
            lax.fori_loop(first, last, go, 0)

    local(small_ref.at[f], got_ref.at[f], 0)

    def send_slices(k, carry):
        d = lax.rem(f + k, peers)
        remote(small_ref.at[d], got_ref.at[f], 0, (x, d))
        return carry

    lax.fori_loop(1, peers, send_slices, 0)

    band, place = f // 16, f % 16

    @pl.when(x == 0)
    def _():
        def send_old(k, carry):
            i = lax.rem(f + k, peers)
            src = turned_ref.at[:, i // 4, :, lanes(i % 4)]
            dst = old_ref.at[pl.ds(2 * place, 2)]
            self_ = jnp.logical_and(band == 0, i == f)

            @pl.when(self_)
            def _():
                local(src, dst, 1)

            @pl.when(jnp.logical_not(self_))
            def _():
                remote(src, dst, 1, (band, i))

            return carry

        lax.fori_loop(0, peers, send_old, 0)

    send_blocks("start")
    local(big_ref.at[f], arrived_ref.at[f], 11)
    local(front_ref, rest_ref, 12)
    wait(got_ref, 1, 0)
    wait(old_ref, 1, 1)

    slot = got_ref[:, 8, :]
    want = (2 * lax.broadcasted_iota(jnp.int32, (peers, tile), 1) + q % 2).astype(jnp.float32)
    pick = jnp.where(slot == want, 1.0, 0.0)
    for r in range(8):
        add = dot(pick, got_ref[:, r, :], 0, 0)
        part_ref[:, r, :] = old_ref[:, r, :] + add[0:32]

    panel_mine = panel_ref.at[:, z, half, :, lanes(q)]
    diag_mine = diag_ref.at[:, z, half, :, lanes(q)]

    @pl.when(x == 0)
    def _():
        local(part_ref.at[0:4], diag_mine, 3)

        def send_x(k, carry):
            remote(part_ref.at[0:4], diag_mine, 3, (k, f))
            return carry

        lax.fori_loop(1, leafs, send_x, 0)

    local(part_ref, panel_mine, 2)
    label_ref[...] = got_ref[:, 9, :].astype(jnp.int32)
    wait(diag_mine, 1, 3)

    def along_z(ref, stage):
        def go(k, carry):
            view = ref.at[:, z, half, :, lanes(q)]
            remote(view, view, stage, (x, device(lax.rem(z + k, NZ), y, c)))
            return carry

        lax.fori_loop(1, NZ, go, 0)

    def along_y(ref, stage):
        def go(k, carry):
            view = ref.at[:, :, half, :, lanes(q)]
            remote(view, view, stage, (x, device(z, lax.rem(y + k, NY), c)))
            return carry

        lax.fori_loop(1, NY, go, 0)

    def across(ref, stage):
        for h in range(2):
            view = ref.at[:, :, :, :, lanes(2 * h + c)]
            remote(view, view, stage, (x, device(z, y, 1 - c)))

    def views(ref, axis):
        if axis == 0:
            return ref.at[:, pl.ds(0, NZ - 1), half, :, lanes(q)]
        if axis == 1:
            return ref.at[:, :, 0, :, pl.ds(0, (NY - 1) * tile)]
        return ref.at[:, :, :, :, pl.ds(0, 2 * tile)]

    along_z(diag_ref, 4)
    wait(panel_mine, 1, 2)
    along_z(panel_ref, 5)
    send_blocks("dz")
    wait(views(diag_ref, 0), 1, 4)
    along_y(diag_ref, 6)
    send_blocks("dy")
    wait(views(diag_ref, 1), 1, 6)
    across(diag_ref, 8)
    wait(views(panel_ref, 0), 1, 5)
    along_y(panel_ref, 7)
    send_blocks("py")
    wait(views(diag_ref, 2), 1, 8)

    rows = panel_ref.at[pl.ds(2 * place, 2)]

    def hook0():
        send_blocks("h0")

    def hook1():
        send_blocks("h1")

    def hook2():
        send_blocks("h2")

    def hook3():
        wait(views(panel_ref, 1), 1, 7)
        across(panel_ref, 9)
        send_blocks("h3")
        wait(views(panel_ref, 2), 1, 9)

        @pl.when(x == band)
        def _():
            local(rows, mine_ref, 10)

            def send_rows(k, carry):
                remote(rows, mine_ref, 10, (lax.rem(x + k, leafs), f))
                return carry

            lax.fori_loop(1, leafs, send_rows, 0)

        wait(mine_ref, 1, 10)

    d2 = diag_ref.reshape(512, 512)
    low = panel_inverses(d2, m_ref, p_ref, q_ref, c1_ref, c2_ref, (hook0, hook1, hook2, hook3))
    panel_weights(f, low, c1_ref, c2_ref, mine_ref.reshape(256, 512), high_ref, low_ref)
    wait(rest_ref, 1, 12)
    x2 = panel_ref.reshape(4096, 512)

    def subtract(step, carry):
        kind = jnp.where(x == 0, jnp.minimum(step, 2), 2)
        at = pl.ds(pl.multiple_of(step * 256, 256), 256)
        minus = product(x2[at, :], (high_ref[kind], low_ref[kind]))
        keep = jnp.logical_or(f >= 2, jnp.logical_and(f == 1, kind == 0))
        rest_ref[at, :] = jnp.where(keep, rest_ref[at, :], 0.0) - minus
        return carry

    lax.fori_loop(0, 16, subtract, 0)

    wait(small_ref.at[pl.ds(0, peers - 1)], 0, 0)

    @pl.when(x == 0)
    def _():
        @pl.when(band == 0)
        def _():
            wait(turned_ref.at[:, pl.ds(0, 15), :, :], 0, 1)
            wait(turned_ref.at[:, 0, :, pl.ds(0, 3 * tile)], 0, 1)

        @pl.when(band != 0)
        def _():
            wait(turned_ref, 0, 1)

        wait(part_ref.at[pl.ds(0, 4 * (leafs - 1))], 0, 3)

    wait(views(diag_ref, 0), 0, 4)
    wait(views(panel_ref, 0), 0, 5)
    wait(views(diag_ref, 1), 0, 6)
    wait(views(panel_ref, 1), 0, 7)
    wait(views(diag_ref, 2), 0, 8)
    wait(views(panel_ref, 2), 0, 9)

    @pl.when(x == band)
    def _():
        wait(panel_ref.at[pl.ds(0, 2 * (leafs - 1))], 0, 10)

    wait(big_ref.at[pl.ds(0, peers - 1)], 0, 11)
    wait(arrived_ref, 1, 11)


PLAN = {"py": (1, 22), "h0": (22, 43), "h1": (43, 64)}


def panels(mesh_shape, big, small, turned, front):
    f32, bf16 = jnp.float32, jnp.bfloat16
    leafs, peers = mesh_shape["leaf"], mesh_shape["front"]
    vm = pl.BlockSpec(memory_space=pltpu.VMEM)
    hbm = pl.BlockSpec(memory_space=pl.ANY)
    return pl.pallas_call(
        functools.partial(panel_kernel, leafs, PLAN),
        out_shape=(
            jax.ShapeDtypeStruct(front.shape, f32),
            jax.ShapeDtypeStruct(big.shape, f32),
            jax.ShapeDtypeStruct((peers, 128), jnp.int32),
        ),
        in_specs=[hbm, vm, vm, hbm],
        out_specs=(vm, hbm, vm),
        scratch_shapes=[
            pltpu.VMEM((32, NZ, 2, 8, 512), f32),
            pltpu.VMEM((4, NZ, 2, 8, 512), f32),
            pltpu.VMEM((2, NZ, 2, 8, 512), f32),
            pltpu.VMEM((peers, 16, 128), f32),
            pltpu.VMEM((32, 8, 128), f32),
            pltpu.VMEM((32, 8, 128), f32),
            pltpu.VMEM((3, 512, 256), bf16),
            pltpu.VMEM((3, 512, 256), bf16),
            pltpu.VMEM((128, 256), f32),
            pltpu.VMEM((128, 128), f32),
            pltpu.VMEM((128, 128), f32),
            pltpu.VMEM((256, 256), f32),
            pltpu.VMEM((256, 256), f32),
            pltpu.SemaphoreType.DMA((2, 13)),
        ],
        compiler_params=pltpu.CompilerParams(has_side_effects=True, collective_id=0),
        name="panels",
    )(big, small, turned.reshape(2, 16, 8, 512), front)


def dot(a, b, ca=1, cb=0):
    return lax.dot_general(a, b, (((ca,), (cb,)), ((), ())), precision=HI, preferred_element_type=jnp.float32)


def factor_inverse(a, m_ref, out_ref):
    n = 128
    row = lax.broadcasted_iota(jnp.int32, (n, n), 0)
    col = lax.broadcasted_iota(jnp.int32, (n, n), 1)
    m_ref[:, 0:n] = a
    m_ref[:, n : 2 * n] = jnp.where(row == col, 1.0, 0.0)
    sub = lax.broadcasted_iota(jnp.int32, (8, n), 0)
    lane = lax.broadcasted_iota(jnp.int32, (8, n), 1)

    def group(g, carry):
        start = pl.multiple_of(g * 8, 8)
        left = m_ref[pl.ds(start, 8), 0:n]
        right = m_ref[pl.ds(start, 8), n : 2 * n]
        cols = [jnp.broadcast_to(left[:, k : k + 1], (8, n)) for k in range(8)]
        scale = jnp.ones((8, n), jnp.float32)
        for j in range(8):
            pivot = jnp.broadcast_to(cols[j][j : j + 1, :], (8, n))
            below = jnp.where(sub > j, cols[j], 0.0) / pivot
            scale = jnp.where(sub == j, pivot, scale)
            for k in range(j + 1, 8):
                cols[k] = cols[k] - below * jnp.broadcast_to(cols[k][j : j + 1, :], (8, n))
            left = left - below * jnp.broadcast_to(left[j : j + 1, :], (8, n))
            right = right - below * jnp.broadcast_to(right[j : j + 1, :], (8, n))
        scale = lax.rsqrt(scale)
        left = left * scale
        right = right * scale
        out_ref[pl.ds(start, 8), :] = right
        turned = pltpu.roll(left, start, axis=1)
        turned = jnp.where(lane >= start + 8, turned, 0.0)
        m_ref[:, 0:n] = pltpu.roll(m_ref[:, 0:n] - dot(turned, left, 0, 0), n - 8, axis=1)
        m_ref[:, n : 2 * n] = m_ref[:, n : 2 * n] - dot(turned, right, 0, 0)
        return carry

    lax.fori_loop(0, n // 8, group, 0)


def factor_inverse_256(a, m_ref, p_ref, q_ref, out_ref, between):
    n = 128
    factor_inverse(a[:n, :n], m_ref, p_ref)
    between()
    p = p_ref[...]
    low = dot(a[n:, :n], p, 1, 1)
    factor_inverse(a[n:, n:] - dot(low, low, 1, 1), m_ref, q_ref)
    q = q_ref[...]
    out_ref[:n, :n] = p
    out_ref[:n, n:] = jnp.zeros((n, n), jnp.float32)
    out_ref[n:, n:] = q
    out_ref[n:, :n] = -dot(q, dot(low, p))


def panel_inverses(d_ref, m_ref, p_ref, q_ref, c1_ref, c2_ref, hooks):
    w = 256
    d11 = d_ref[0:w, 0:w]
    factor_inverse_256(0.5 * (d11 + d11.T), m_ref, p_ref, q_ref, c1_ref, hooks[0])
    hooks[1]()
    low = dot(d_ref[w:, 0:w], c1_ref[...], 1, 1)
    d22 = d_ref[w:, w:] - dot(low, low, 1, 1)
    factor_inverse_256(0.5 * (d22 + d22.T), m_ref, p_ref, q_ref, c2_ref, hooks[2])
    hooks[3]()
    return low


def panel_weights(column, low, c1_ref, c2_ref, xc_ref, high_ref, low_ref):
    w = 256
    c1 = c1_ref[...]
    c2 = c2_ref[...]
    b = dot(c1, low, 0, 1)
    lc1 = dot(xc_ref[:, 0:w], c1, 1, 1)
    lc2 = dot(xc_ref[:, w:] - dot(lc1, low, 1, 1), c2, 1, 1)
    w1 = dot(c1, lc1, 0, 1)
    w2 = dot(c2, lc2, 0, 1)
    row = lax.broadcasted_iota(jnp.int32, (w, w), 0)
    col = lax.broadcasted_iota(jnp.int32, (w, w), 1)
    eye = jnp.where(row == col, 1.0, 0.0)
    first = column == 0
    second = column == 1
    c1t = dot(c1, eye, 0, 0)
    c2t = dot(c2, eye, 0, 0)
    w1 = jnp.where(first, -c1t, w1)
    w2 = jnp.where(second, -c2t, w2)
    none = jnp.zeros((w, w), jnp.float32)

    def put(kind, rows, value):
        high_ref[kind, rows, :], low_ref[kind, rows, :] = split(value)

    w2 = jnp.where(first, none, w2)
    top = jnp.where(first, w1, jnp.where(second, -dot(b, w2), w1 - dot(b, w2)))
    put(0, slice(0, w), jnp.where(first, w1, none))
    put(0, slice(w, 2 * w), none)
    put(1, slice(0, w), jnp.where(second, top, w1))
    put(1, slice(w, 2 * w), jnp.where(second, w2, none))
    put(2, slice(0, w), top)
    put(2, slice(w, 2 * w), w2)


def shards(mesh_shape, front, updates, target_owner, target_slot):
    peers = mesh_shape["front"]
    big, small, turned = sort_blocks(target_owner, target_slot, updates, front, peers)
    rest, arrived, labels = panels(mesh_shape, big, small, turned, front)
    return finish(labels, rest, arrived)


def solution(mesh):
    return jax.shard_map(
        functools.partial(shards, dict(mesh.shape)),
        mesh=mesh,
        in_specs=(
            P("leaf", "front"),
            P(("leaf", "front"), None, None),
            P(("leaf", "front")),
            P(("leaf", "front")),
        ),
        out_specs=P("leaf", "front"),
        check_vma=False,
    )
```
